128 devices in a mesh: section: 4 (over z), row: 8 (over x, core), col: 4 (over y).
Axes of the slice: x: 4, y: 4, z: 4, core: 2. Of those that a mesh axis runs over, the one named last changes fastest.
Arguments:
- tokens: bfloat16 [4, 512, 4096], P('section', 'col', 'row'), may hold values from -6 to 6
- cotangent: bfloat16 [4, 512, 4096], P('section', 'col', 'row'), may hold values from -6 to 6
- noised: int32 [4, 512], P('section', 'col'), may hold values from 0 to 1, as said below
- gate_weight: bfloat16 [4, 4096, 16384], P('section', None, ('row', 'col')), may hold values from -0.09375 to 0.09375
- up_weight: bfloat16 [4, 4096, 16384], P('section', None, ('row', 'col')), may hold values from -0.09375 to 0.09375
- down_weight: bfloat16 [4, 16384, 4096], P('section', ('row', 'col')), may hold values from -0.046875 to 0.046875
- block_keep: int32 [4, 3, 32, 128], P('section', None, None, ('row', 'col')), may hold values 0 or 1
Outputs:
- grad_gate: bfloat16 [4, 4096, 16384], P('section', None, ('row', 'col'))
- grad_up: bfloat16 [4, 4096, 16384], P('section', None, ('row', 'col'))
- grad_down: bfloat16 [4, 16384, 4096], P('section', ('row', 'col'))
- handoff: bfloat16 [4, 512, 4096], P('section', 'col')
The draws below stay inside these ranges and needn't reach their ends.
Inputs may be any that keep to these rules, and one draw needn't show every extreme that they name: Each aligned block of 128 tokens of a section (the tokens of one grid column) holds 1 to 96 noised tokens; in every section some block holds exactly 96.
All inputs are finite; a program needn't handle non-finite values. No bound on the sum of `block_keep` on one device may be relied on, other than what follows from the above.
Results may differ from the reference program's by a relative error of at most 0.0051.
Values may be sent and summed in bfloat16 or wider, within the bound.
No kernel may reach another device: no remote copies, remote signals or barrier semaphores. Data moves between devices by JAX's collectives and lax.ppermute only.
A program may use at most 128 MiB of HBM per device.

```python
import jax
import jax.numpy as jnp
from jax import lax

D = 4096
FF = 16384
TOK_DEV = 128
CAP = 96
TOKENS = 512
N_SECTION = 4


def draw_noised(key, part):
    blocks_count = TOKENS // TOK_DEV
    sections_count = N_SECTION
    base = jax.random.fold_in(key, 17)
    first_key, second_key, third_key = jax.random.split(base, 3)
    counts = jax.random.randint(first_key, (sections_count, blocks_count), 1, CAP + 1)
    fullest = jax.random.randint(second_key, (sections_count, 1), 0, blocks_count)
    counts = jnp.where(jnp.arange(blocks_count)[None, :] == fullest, CAP, counts)
    block_keys = jax.random.split(third_key, sections_count * blocks_count)
    ranking = jax.vmap(lambda single: jax.random.permutation(single, TOK_DEV))(block_keys)
    ranking = ranking.reshape(sections_count, blocks_count, TOK_DEV)
    chosen = (ranking < counts[:, :, None]).astype(jnp.int32)
    return chosen.reshape(sections_count, TOKENS)


def set_ends(result, stream_key, least, high):
    shape = result.shape
    spot = [jax.random.randint(jax.random.fold_in(stream_key, axis), (), 0, shape[axis]) for axis in range(len(shape))]
    result = result.at[tuple(spot)].set(least)
    longest = shape.index(max(shape))
    spot[longest] = (spot[longest] + 1) % shape[longest]
    return result.at[tuple(spot)].set(high)


def level_of(stream_key, extent, shards, smallest, largest):
    level = 1.0
    for dim, shards_of in shards:
        steps = jax.random.uniform(jax.random.fold_in(jax.random.fold_in(stream_key, 6), dim), (shards_of,), jnp.float32, smallest / len(shards), largest / len(shards))
        level = level * jnp.repeat(jnp.exp(steps), extent[dim] // shards_of).reshape((-1,) + (1,) * (len(extent) - 1 - dim))
    return level


def centred(stream_key, shape, spread, most, cuts=(), held_as=jnp.bfloat16):
    drawn = spread * jax.random.normal(stream_key, shape, jnp.float32)
    if cuts:
        drawn = drawn * level_of(stream_key, shape, cuts, -0.22, 0.18)
    return jnp.clip(drawn, -most, most).astype(held_as)


def setup_inputs(seed: int = 0) -> dict:
    streams_of = jax.random.split(jax.random.key(seed), 8)
    return {
        "tokens": centred(streams_of[0], (N_SECTION, TOKENS, D), 1.0, 6.0, ((0, 4), (1, 4), (2, 8))),
        "cotangent": centred(streams_of[1], (N_SECTION, TOKENS, D), 1.0, 6.0, ((0, 4), (1, 4), (2, 8))),
        "noised": draw_noised(jax.random.fold_in(streams_of[7], 71), 0),
        "gate_weight": centred(streams_of[3], (N_SECTION, D, FF), D ** -0.5, 0.09375, ((0, 4), (2, 32))),
        "up_weight": centred(streams_of[4], (N_SECTION, D, FF), D ** -0.5, 0.09375, ((0, 4), (2, 32))),
        "down_weight": centred(streams_of[5], (N_SECTION, FF, D), FF ** -0.5, 0.046875, ((0, 4), (1, 32))),
        "block_keep": set_ends((jax.random.randint(streams_of[6], (N_SECTION, 3, D // 128, FF // 128), 0, 2) < 1).astype(jnp.int32), jax.random.fold_in(streams_of[6], 1), 0, 1),
    }


def expand_blocks(block_mask, block_edge):
    widened = jnp.repeat(jnp.repeat(block_mask, block_edge, axis=0), block_edge, axis=1)
    return widened.astype(jnp.bfloat16)


def contract_rows(left, right):
    return lax.dot_general(left, right, (((0,), (0,)), ((), ())), preferred_element_type=jnp.float32)


def contract_cols(left, right):
    return lax.dot_general(left, right, (((1,), (1,)), ((), ())), preferred_element_type=jnp.float32)


def layer_grads(tokens, cotangent, noised, gate_weight, up_weight, down_weight, block_keep):
    gate_mask = expand_blocks(block_keep[0], 128)
    up_mask = expand_blocks(block_keep[1], 128)
    down_mask = expand_blocks(block_keep[2].T, 128)
    gate_eff = gate_weight * gate_mask
    up_eff = up_weight * up_mask
    down_eff = down_weight * down_mask
    masked_cot = cotangent * noised[:, None].astype(jnp.bfloat16)
    gate_pre = jnp.dot(tokens, gate_eff, preferred_element_type=jnp.float32)
    up_pre = jnp.dot(tokens, up_eff, preferred_element_type=jnp.float32)
    sigmoid_gate = jax.nn.sigmoid(gate_pre)
    silu_gate = gate_pre * sigmoid_gate
    hidden = (silu_gate * up_pre).astype(jnp.bfloat16)
    grad_hidden = contract_cols(masked_cot, down_eff)
    grad_down = (contract_rows(hidden, masked_cot) * down_mask).astype(jnp.bfloat16)
    grad_gate_pre = (grad_hidden * up_pre * sigmoid_gate * (1.0 + gate_pre * (1.0 - sigmoid_gate))).astype(jnp.bfloat16)
    grad_up_pre = (grad_hidden * silu_gate).astype(jnp.bfloat16)
    grad_gate = (contract_rows(tokens, grad_gate_pre) * gate_mask).astype(jnp.bfloat16)
    grad_up = (contract_rows(tokens, grad_up_pre) * up_mask).astype(jnp.bfloat16)
    grad_input = (contract_cols(grad_gate_pre, gate_eff) + contract_cols(grad_up_pre, up_eff)).astype(jnp.bfloat16)
    return grad_gate, grad_up, grad_down, grad_input


def reference(tokens, cotangent, noised, gate_weight, up_weight, down_weight, block_keep):
    results = []
    for section_index in range(tokens.shape[0]):
        results.append(layer_grads(tokens[section_index], cotangent[section_index], noised[section_index],
                                   gate_weight[section_index], up_weight[section_index],
                                   down_weight[section_index], block_keep[section_index]))
    grad_gate = jnp.stack([entry[0] for entry in results])
    grad_up = jnp.stack([entry[1] for entry in results])
    grad_down = jnp.stack([entry[2] for entry in results])
    inputs_grad = jnp.stack([entry[3] for entry in results])
    handoff = jnp.concatenate([inputs_grad[1:], jnp.zeros_like(inputs_grad[:1])], axis=0)
    return grad_gate, grad_up, grad_down, handoff
```

```python
import functools

import jax
import jax.numpy as jnp
from jax import lax
from jax.experimental import pallas as pl
from jax.experimental.pallas import tpu as pltpu
from jax.sharding import PartitionSpec as P


BF = jnp.bfloat16
F32 = jnp.float32
CAP = 96
SHIFTS = (0, 1, -1, 2)
ANY = pl.BlockSpec(memory_space=pl.ANY)
VM = pl.BlockSpec(memory_space=pltpu.VMEM)


def cost(flops, nbytes):
    return pl.CostEstimate(flops=int(flops), bytes_accessed=int(nbytes), transcendentals=0)


def params(**kw):
    return pltpu.CompilerParams(**kw)


def phase(array, which, by):
    pairs = []
    for x in range(4):
        for core in range(2):
            for y in range(4):
                along_x = (core == 0) == (which == 0)
                tx, ty = ((x + by) % 4, y) if along_x else (x, (y + by) % 4)
                pairs.append(((x * 2 + core) * 4 + y, (tx * 2 + core) * 4 + ty))
    return lax.ppermute(array, ("row", "col"), pairs)


def swap_cores(array):
    return lax.ppermute(array, "row", [(i, i ^ 1) for i in range(8)])


def along_x(array, by):
    return lax.ppermute(array, "row", [(i, (i + 2 * by) % 8) for i in range(8)])


def to_preceding(array):
    return lax.ppermute(array, "section", [(i, i - 1) for i in range(1, 4)])


def selector(noised):
    flags = noised.astype(F32)
    lower = lax.broadcasted_iota(jnp.int32, (128, 128), 0) <= lax.broadcasted_iota(jnp.int32, (128, 128), 1)
    rank = jnp.dot(
        jnp.broadcast_to(flags, (16, 128)).astype(BF), lower.astype(F32).astype(BF), preferred_element_type=F32
    )[0:1]
    slot = lax.broadcasted_iota(jnp.int32, (CAP, 128), 0).astype(F32) + 1.0
    return jnp.where(jnp.logical_and(slot == rank, flags > 0.5), 1.0, 0.0).astype(BF)


def compact_kernel(noised, tokens, cotangent, own):
    pick = selector(noised[...])
    own[0] = jnp.dot(pick, tokens[...], preferred_element_type=F32).astype(BF)
    own[1] = jnp.dot(pick, cotangent[...], preferred_element_type=F32).astype(BF)


def masked(weight, keep, which, model_block, transposed=False):
    rows = []
    for i in range(4):
        cols = []
        for j in range(4):
            f, h = (j, i) if transposed else (i, j)
            flag = keep[(which * 32 + model_block * 4 + f) * 4 + h].astype(F32).astype(BF)
            cols.append(weight[i * 128 : (i + 1) * 128, j * 128 : (j + 1) * 128] * flag)
        rows.append(jnp.concatenate(cols, axis=1))
    return jnp.concatenate(rows, axis=0)


def forward_kernel(
    place, keep, g0, g1, g2, g3, h0, h1, h2, h3, wg, wu, wd,
    ggp, gup, hid, xa, ca, xs, cs, acc_g, acc_u, acc_h, sem_x, sem_c, sem_o,
):
    step = pl.program_id(0)
    x, core, y = place[0], place[1], place[2]

    @pl.when(step == 0)
    def _():
        for other, arrays in ((0, (g0, g1, g2, g3)), (1, (h0, h1, h2, h3))):
            parity = core ^ other
            for i in range(4):
                for j in range(4):
                    first, second = SHIFTS[j], SHIFTS[i]
                    bx = lax.rem(x + 4 - jnp.where(parity == 0, first, second), 4)
                    by = lax.rem(y + 4 - jnp.where(parity == 0, second, first), 4)
                    r = bx * 2 + parity
                    rows = pl.ds(pl.multiple_of(by * CAP, CAP), CAP)
                    pltpu.make_async_copy(arrays[i].at[j, 0], xs.at[r, rows], sem_x.at[r]).start()
                    pltpu.make_async_copy(arrays[i].at[j, 1], cs.at[r, rows], sem_c.at[r]).start()

    pltpu.make_async_copy(xa.at[step], xs.at[step], sem_x.at[step]).wait()
    pltpu.make_async_copy(ca.at[step], cs.at[step], sem_c.at[step]).wait()
    out_x = pltpu.make_async_copy(xs.at[step], xa.at[step], sem_o.at[0, step])
    out_c = pltpu.make_async_copy(cs.at[step], ca.at[step], sem_o.at[1, step])
    out_x.start()
    out_c.start()
    xb, cb = xs[step], cs[step]
    pg = jnp.dot(xb, masked(wg, keep, 0, step), preferred_element_type=F32)
    pu = jnp.dot(xb, masked(wu, keep, 1, step), preferred_element_type=F32)
    ph = lax.dot_general(
        cb, masked(wd, keep, 2, step, True), (((1,), (1,)), ((), ())), preferred_element_type=F32
    )

    @pl.when(step == 0)
    def _():
        acc_g[...], acc_u[...], acc_h[...] = pg, pu, ph

    @pl.when(step > 0)
    def _():
        acc_g[...] += pg
        acc_u[...] += pu
        acc_h[...] += ph

    @pl.when(step == 7)
    def _():
        g, u, gh = acc_g[...], acc_u[...], acc_h[...]
        sig = 1.0 / (1.0 + jnp.exp(-g))
        silu = g * sig
        hid[...] = (silu * u).astype(BF)
        ggp[...] = (gh * u * sig * (1.0 + g * (1.0 - sig))).astype(BF)
        gup[...] = (gh * silu).astype(BF)
        for r in range(8):
            pltpu.make_async_copy(xs.at[r], xa.at[r], sem_o.at[0, r]).wait()
            pltpu.make_async_copy(cs.at[r], ca.at[r], sem_o.at[1, r]).wait()


def input_block(ggp, gup, wg, wu, keep, block):
    dims = (((1,), (1,)), ((), ()))
    return lax.dot_general(
        ggp[...], masked(wg, keep, 0, block), dims, preferred_element_type=F32
    ) + lax.dot_general(gup[...], masked(wu, keep, 1, block), dims, preferred_element_type=F32)


def partner_kernel(place, keep, ggp, gup, wg, wu, out):
    block = (1 - place[1]) * 4 + pl.program_id(0)
    out[0] = input_block(ggp, gup, wg, wu, keep, block).astype(BF)


def own_kernel(place, keep, ggp, gup, wg, wu, recv, o0, o1, o2, o3, full, half, sem):
    q = pl.program_id(0)
    x, core, y = place[0], place[1], place[2]
    total = input_block(ggp, gup, wg, wu, keep, core * 4 + q) + recv[0].astype(F32)
    full[q] = total
    half[q] = total.astype(BF)

    @pl.when(q == 3)
    def _():
        copies = []
        for i, out in enumerate((o0, o1, o2, o3)):
            for t in range(4):
                qq = jnp.where(core == 0, lax.rem(x + 4 + SHIFTS[i], 4), t)
                c = jnp.where(core == 0, t, lax.rem(y + 4 + SHIFTS[i], 4))
                rows = pl.ds(pl.multiple_of(c * CAP, CAP), CAP)
                source = full if i == 0 else half
                copies.append(pltpu.make_async_copy(source.at[qq, rows], out.at[t], sem.at[i, t]))
        for copy in copies:
            copy.start()
        for copy in copies:
            copy.wait()


def sum_kernel(place, own, r1, r2, r3, o0, o1, o2, o3):
    base = jnp.where(place[1] == 0, place[2], place[0])
    for shift, out in zip(SHIFTS, (o0, o1, o2, o3)):
        t = lax.rem(base + 4 + shift, 4)
        total = own[t] + r1[t].astype(F32) + r2[t].astype(F32) + r3[t].astype(F32)
        out[...] = total.astype(out.dtype)


def expand_kernel(place, noised, t0, t1, t2, t3, u0, u1, u2, u3, out):
    pick = selector(noised[...])
    x, core = place[0], place[1]
    for other, tiles in ((0, (t0, t1, t2, t3)), (1, (u0, u1, u2, u3))):
        for shift, tile in zip(SHIFTS, tiles):
            column = ((core ^ other) * 4 + lax.rem(x + 4 - shift, 4)) * 512
            out[:, pl.ds(pl.multiple_of(column, 512), 512)] = lax.dot_general(
                pick, tile[...], (((0,), (0,)), ((), ())), preferred_element_type=F32
            ).astype(BF)


def gate_up_kernel(keep, xa, ggp, gup, gg, gu):
    r = pl.program_id(0)
    dims = (((0,), (0,)), ((), ()))
    for which, grad, out in ((0, ggp, gg), (1, gup, gu)):
        value = lax.dot_general(xa[0], grad[...], dims, preferred_element_type=F32).astype(BF)
        out[...] = masked(value, keep, which, r)


def down_kernel(keep, ca, hid, gd):
    r = pl.program_id(0)
    value = lax.dot_general(
        hid[...], ca[0], (((0,), (0,)), ((), ())), preferred_element_type=F32
    ).astype(BF)
    gd[...] = masked(value, keep, 2, r, True)


def shaped(shape, dtype=BF):
    return jax.ShapeDtypeStruct(shape, dtype)


def on_device(tokens, cotangent, noised, gate_weight, up_weight, down_weight, block_keep):
    row = lax.axis_index("row")
    place = jnp.stack([row // 2, row % 2, lax.axis_index("col")]).astype(jnp.int32)
    keep = block_keep.reshape(-1)
    wg, wu, wd = gate_weight[0], up_weight[0], down_weight[0]
    rows = 4 * CAP
    next_noised = to_preceding(noised.astype(F32))

    own = pl.pallas_call(
        compact_kernel, out_shape=shaped((2, CAP, 512)), in_specs=[VM] * 3, out_specs=VM,
        cost_estimate=cost(5e7, 5e5), name="compact",
    )(noised, tokens[0], cotangent[0])
    first = [own] + [phase(own, 0, d) for d in SHIFTS[1:]]
    packed = jnp.stack(first)
    gathered = [packed] + [phase(packed, 1, d) for d in SHIFTS[1:]]
    swapped = [swap_cores(g) for g in gathered]

    w_spec = pl.BlockSpec((512, 512), lambda s, *_: (s, 0))
    d_spec = pl.BlockSpec((512, 512), lambda s, *_: (0, s))
    whole = pl.BlockSpec((rows, 512), lambda s, *_: (0, 0))
    ggp, gup, hid, xa, ca = pl.pallas_call(
        forward_kernel,
        out_shape=[shaped((rows, 512))] * 3 + [shaped((8, rows, 512))] * 2,
        grid_spec=pltpu.PrefetchScalarGridSpec(
            num_scalar_prefetch=2, grid=(8,),
            in_specs=[ANY] * 8 + [w_spec, w_spec, d_spec],
            out_specs=[whole] * 3 + [ANY] * 2,
            scratch_shapes=[pltpu.VMEM((8, rows, 512), BF)] * 2 + [pltpu.VMEM((rows, 512), F32)] * 3
            + [pltpu.SemaphoreType.DMA((8,))] * 2 + [pltpu.SemaphoreType.DMA((2, 8))],
        ),
        cost_estimate=cost(4.8e9, 2.4e7), name="forward",
    )(place, keep, *gathered, *swapped, wg, wu, wd)

    part = functools.partial(pltpu.PrefetchScalarGridSpec, num_scalar_prefetch=2, grid=(4,))
    block = pl.BlockSpec((1, rows, 512), lambda s, *_: (s, 0, 0))
    theirs = pl.BlockSpec((512, 512), lambda s, p, k: ((1 - p[1]) * 4 + s, 0))
    ours = pl.BlockSpec((512, 512), lambda s, p, k: (p[1] * 4 + s, 0))
    partner = pl.pallas_call(
        partner_kernel, out_shape=shaped((4, rows, 512)),
        grid_spec=part(in_specs=[whole, whole, theirs, theirs], out_specs=block),
        cost_estimate=cost(1.6e9, 6.5e6), name="partner",
    )(place, keep, ggp, gup, wg, wu)
    recv = swap_cores(partner)
    outs = pl.pallas_call(
        own_kernel, out_shape=[shaped((4, CAP, 512), F32)] + [shaped((4, CAP, 512))] * 3,
        grid_spec=part(
            in_specs=[whole, whole, ours, ours, block], out_specs=[ANY] * 4,
            scratch_shapes=[pltpu.VMEM((4, rows, 512), F32), pltpu.VMEM((4, rows, 512), BF),
                            pltpu.SemaphoreType.DMA((4, 4))],
        ),
        cost_estimate=cost(1.6e9, 8e6), name="own",
    )(place, keep, ggp, gup, wg, wu, recv)
    got = [phase(o, 0, d) for o, d in zip(outs[1:], SHIFTS[1:])]
    tiles = pl.pallas_call(
        sum_kernel, out_shape=[shaped((CAP, 512), F32)] + [shaped((CAP, 512))] * 3,
        in_specs=[pl.BlockSpec(memory_space=pltpu.SMEM)] + [VM] * 4, out_specs=[VM] * 4,
        cost_estimate=cost(1e6, 2.5e6), name="sum",
    )(place, outs[0], *got)
    got = [phase(o, 1, d) for o, d in zip(tiles[1:], SHIFTS[1:])]
    share = (tiles[0] + sum(g.astype(F32) for g in got)).astype(BF)
    share = to_preceding(share)
    strip = [share] + [along_x(share, d) for d in SHIFTS[1:]]
    handoff = pl.pallas_call(
        expand_kernel, out_shape=shaped((128, 4096)),
        in_specs=[pl.BlockSpec(memory_space=pltpu.SMEM)] + [VM] * 9, out_specs=VM,
        cost_estimate=cost(1e8, 2e6), name="expand",
    )(place, next_noised, *strip, *[swap_cores(t) for t in strip])

    each = functools.partial(pltpu.PrefetchScalarGridSpec, num_scalar_prefetch=1, grid=(8,))
    pane = pl.BlockSpec((1, rows, 512), lambda s, *_: (s, 0, 0))
    grad_gate, grad_up = pl.pallas_call(
        gate_up_kernel, out_shape=[shaped((4096, 512))] * 2,
        grid_spec=each(in_specs=[pane, whole, whole], out_specs=[w_spec, w_spec]),
        cost_estimate=cost(3.2e9, 1.2e7), name="gate_up",
    )(keep, xa, ggp, gup)
    grad_down = pl.pallas_call(
        down_kernel, out_shape=shaped((512, 4096)),
        grid_spec=each(in_specs=[pane, whole], out_specs=d_spec),
        cost_estimate=cost(1.6e9, 8e6), name="down",
    )(keep, ca, hid)
    return (grad_gate[None], grad_up[None], grad_down[None], handoff[None])


def solution(mesh):
    placed = (
        P("section", "col", "row"),
        P("section", "col", "row"),
        P("section", "col"),
        P("section", None, ("row", "col")),
        P("section", None, ("row", "col")),
        P("section", ("row", "col"), None),
        P("section", None, None, ("row", "col")),
    )
    return jax.shard_map(
        on_device,
        mesh=mesh,
        in_specs=placed,
        out_specs=(
            P("section", None, ("row", "col")),
            P("section", None, ("row", "col")),
            P("section", ("row", "col"), None),
            P("section", "col", None),
        ),
        check_vma=False,
    )
```

```python
import jax
import jax.numpy as jnp
from jax import lax
from jax.experimental import pallas as pl
from jax.experimental.pallas import tpu as pltpu
from jax.sharding import PartitionSpec as P


BF = jnp.bfloat16
F32 = jnp.float32
CAP = 96
SHIFTS = (0, 1, -1, 2)
ANY = pl.BlockSpec(memory_space=pl.ANY)
VM = pl.BlockSpec(memory_space=pltpu.VMEM)


def cost(flops, nbytes):
    return pl.CostEstimate(flops=int(flops), bytes_accessed=int(nbytes), transcendentals=0)


def phase(array, which, by):
    pairs = []
    for x in range(4):
        for core in range(2):
            for y in range(4):
                along_x = (core == 0) == (which == 0)
                tx, ty = ((x + by) % 4, y) if along_x else (x, (y + by) % 4)
                pairs.append(((x * 2 + core) * 4 + y, (tx * 2 + core) * 4 + ty))
    return lax.ppermute(array, ("row", "col"), pairs)


def swap_cores(array):
    return lax.ppermute(array, "row", [(i, i ^ 1) for i in range(8)])


def along_x(array, by):
    return lax.ppermute(array, "row", [(i, (i + 2 * by) % 8) for i in range(8)])


def to_preceding(array):
    return lax.ppermute(array, "section", [(i, i - 1) for i in range(1, 4)])


def selector(noised):
    flags = noised.astype(F32)
    lower = lax.broadcasted_iota(jnp.int32, (128, 128), 0) <= lax.broadcasted_iota(jnp.int32, (128, 128), 1)
    rank = jnp.dot(
        jnp.broadcast_to(flags, (16, 128)).astype(BF), lower.astype(F32).astype(BF), preferred_element_type=F32
    )[0:1]
    slot = lax.broadcasted_iota(jnp.int32, (CAP, 128), 0).astype(F32) + 1.0
    return jnp.where(jnp.logical_and(slot == rank, flags > 0.5), 1.0, 0.0).astype(BF)


def compact_kernel(noised, tokens, cotangent, own):
    pick = selector(noised[...])
    own[0] = jnp.dot(pick, tokens[...], preferred_element_type=F32).astype(BF)
    own[1] = jnp.dot(pick, cotangent[...], preferred_element_type=F32).astype(BF)


def masked(weight, keep, which, model_block, transposed=False):
    rows = []
    for i in range(4):
        cols = []
        for j in range(4):
            f, h = (j, i) if transposed else (i, j)
            flag = keep[which, h, model_block * 4 + f].astype(F32).astype(BF)
            cols.append(weight[i * 128 : (i + 1) * 128, j * 128 : (j + 1) * 128] * flag)
        rows.append(jnp.concatenate(cols, axis=1))
    return jnp.concatenate(rows, axis=0)


def prepare_kernel(
    place, keep, keep_theirs, wg, wu, wd, wg_theirs, wu_theirs,
    gate, up, mine_t, theirs_t, down_t, in_g, in_u, in_d, in_tg, in_tu, sem,
):
    base = place[1] * 4

    def block(i):
        return pl.ds(pl.multiple_of(i * 512, 512), 512)

    def copies(i):
        return [
            pltpu.make_async_copy(wg.at[block(i)], in_g.at[i], sem.at[0, i]),
            pltpu.make_async_copy(wu.at[block(i)], in_u.at[i], sem.at[1, i]),
            pltpu.make_async_copy(wd.at[:, block(i)], in_d.at[i], sem.at[2, i]),
        ]

    def their_copies(i):
        return [
            pltpu.make_async_copy(wg_theirs.at[block(base + i)], in_tg.at[i], sem.at[3, i]),
            pltpu.make_async_copy(wu_theirs.at[block(base + i)], in_tu.at[i], sem.at[4, i]),
        ]

    for i in range(8):
        for copy in copies(i):
            copy.start()
    for i in range(4):
        for copy in their_copies(i):
            copy.start()

    def step(i, carry):
        for copy in copies(i):
            copy.wait()
        gate[i] = masked(in_g.at[i], keep, 0, i)
        up[i] = masked(in_u.at[i], keep, 1, i)
        down_t[i] = masked(in_d.at[i], keep, 2, i, True).T
        return carry

    lax.fori_loop(0, 8, step, 0)

    def their_step(i, carry):
        for copy in their_copies(i):
            copy.wait()
        mine_t[i, 0:512] = gate[base + i].T
        mine_t[i, 512:1024] = up[base + i].T
        theirs_t[i, 0:512] = masked(in_tg.at[i], keep_theirs, 0, base + i).T
        theirs_t[i, 512:1024] = masked(in_tu.at[i], keep_theirs, 1, base + i).T
        return carry

    lax.fori_loop(0, 4, their_step, 0)


def forward_kernel(place, *refs):
    blocks, (gate, up, down_t, ggup, hid_t, xs, cs), scratch = refs[:16], refs[16:23], refs[23:]
    acc_g, acc_u, acc_h = scratch
    x, core, y = place[0], place[1], place[2]
    for other in range(2):
        parity = core ^ other
        for i in range(4):
            own, others = blocks[other * 8 + i], blocks[other * 8 + 4 + i]
            for j in range(4):
                first, second = SHIFTS[j], SHIFTS[i]
                bx = lax.rem(x + 4 - jnp.where(parity == 0, first, second), 4)
                by = lax.rem(y + 4 - jnp.where(parity == 0, second, first), 4)
                r = bx * 2 + parity
                rows = pl.ds(pl.multiple_of(by * CAP, CAP), CAP)
                xs[r, rows] = own[0] if j == 0 else others[j - 1, 0]
                cs[r, rows] = own[1] if j == 0 else others[j - 1, 1]
    acc_g[...] = jnp.zeros_like(acc_g)
    acc_u[...] = jnp.zeros_like(acc_u)
    acc_h[...] = jnp.zeros_like(acc_h)

    def step(r, carry):
        acc_g[...] += jnp.dot(xs[r], gate[r], preferred_element_type=F32)
        acc_u[...] += jnp.dot(xs[r], up[r], preferred_element_type=F32)
        acc_h[...] += jnp.dot(cs[r], down_t[r], preferred_element_type=F32)
        return carry

    lax.fori_loop(0, 8, step, 0)
    g, u, gh = acc_g[...], acc_u[...], acc_h[...]
    sig = 1.0 / (1.0 + jnp.exp(-g))
    silu = g * sig
    ggup[:, 0:512] = (gh * u * sig * (1.0 + g * (1.0 - sig))).astype(BF)
    ggup[:, 512:1024] = (gh * silu).astype(BF)
    hid_t[...] = (silu * u).astype(BF).T


def mine_kernel(mine, mine_t, out):
    def step(q, carry):
        out[q] = jnp.dot(mine[...], mine_t[q], preferred_element_type=F32)
        return carry

    lax.fori_loop(0, 4, step, 0)


def own_kernel(place, part, theirs, theirs_t, o0, o1, o2, o3, full):
    x, core, y = place[0], place[1], place[2]

    def step(q, carry):
        full[q] = part[q] + jnp.dot(theirs[...], theirs_t[q], preferred_element_type=F32)
        return carry

    lax.fori_loop(0, 4, step, 0)
    for shift, out in zip(SHIFTS, (o0, o1, o2, o3)):
        for t in range(4):
            q = jnp.where(core == 0, lax.rem(x + 4 + shift, 4), t)
            c = jnp.where(core == 0, t, lax.rem(y + 4 + shift, 4))
            out[t] = full[q, pl.ds(pl.multiple_of(c * CAP, CAP), CAP)].astype(out.dtype)


def sum_kernel(place, own, r1, r2, r3, o0, o1, o2, o3):
    base = jnp.where(place[1] == 0, place[2], place[0])
    for shift, out in zip(SHIFTS, (o0, o1, o2, o3)):
        t = lax.rem(base + 4 + shift, 4)
        total = own[t] + r1[t].astype(F32) + r2[t].astype(F32) + r3[t].astype(F32)
        out[...] = total.astype(out.dtype)


def expand_kernel(place, noised, t0, t1, t2, t3, u0, u1, u2, u3, out):
    pick = selector(noised[...])
    x, core = place[0], place[1]
    for other, tiles in ((0, (t0, t1, t2, t3)), (1, (u0, u1, u2, u3))):
        for shift, tile in zip(SHIFTS, tiles):
            column = ((core ^ other) * 4 + lax.rem(x + 4 - shift, 4)) * 512
            out[:, pl.ds(pl.multiple_of(column, 512), 512)] = lax.dot_general(
                pick, tile[...], (((0,), (0,)), ((), ())), preferred_element_type=F32
            ).astype(BF)


def gate_up_kernel(keep, xs, ggup, gg, gu, buf_g, buf_u, sem):
    def copies(r):
        rows = pl.ds(pl.multiple_of(r * 512, 512), 512)
        return [
            pltpu.make_async_copy(buf_g.at[r], gg.at[rows], sem.at[0, r]),
            pltpu.make_async_copy(buf_u.at[r], gu.at[rows], sem.at[1, r]),
        ]

    def step(r, carry):
        value = jnp.dot(xs[r].T, ggup[...], preferred_element_type=F32).astype(BF)
        buf_g[r] = masked(value[:, 0:512], keep, 0, r)
        buf_u[r] = masked(value[:, 512:1024], keep, 1, r)
        for copy in copies(r):
            copy.start()
        return carry

    lax.fori_loop(0, 8, step, 0)
    for r in range(8):
        for copy in copies(r):
            copy.wait()


def down_kernel(keep, cs, hid_t, gd, buf, sem):
    def copy(r):
        return pltpu.make_async_copy(buf.at[r], gd.at[:, pl.ds(pl.multiple_of(r * 512, 512), 512)], sem.at[r])

    def step(r, carry):
        value = jnp.dot(hid_t[...], cs[r], preferred_element_type=F32).astype(BF)
        buf[r] = masked(value, keep, 2, r, True)
        copy(r).start()
        return carry

    lax.fori_loop(0, 8, step, 0)
    for r in range(8):
        copy(r).wait()


def shaped(shape, dtype=BF):
    return jax.ShapeDtypeStruct(shape, dtype)


def hbm(array):
    return pltpu.with_memory_space_constraint(array, pltpu.HBM)


def on_device(tokens, cotangent, noised, gate_weight, up_weight, down_weight, block_keep):
    row = lax.axis_index("row")
    place = jnp.stack([row // 2, row % 2, lax.axis_index("col")]).astype(jnp.int32)
    keep = block_keep[0].transpose(0, 2, 1)
    wg, wu, wd = (hbm(w[0]) for w in (gate_weight, up_weight, down_weight))
    rows = 4 * CAP
    barrier = lax.optimization_barrier
    smem = pl.BlockSpec(memory_space=pltpu.SMEM)

    def room(mib):
        return pltpu.CompilerParams(vmem_limit_bytes=mib << 20)

    own = pl.pallas_call(
        compact_kernel, out_shape=shaped((2, CAP, 512)), in_specs=[VM] * 3, out_specs=VM,
        compiler_params=room(4), cost_estimate=cost(5e7, 5e5), name="compact",
    )(*(hbm(v) for v in (noised, tokens[0], cotangent[0])))
    first = [phase(own, 0, SHIFTS[i]) for i in (1, 2, 3)]
    owns = [own] + [phase(own, 1, SHIFTS[i]) for i in (1, 2, 3)]
    next_noised = to_preceding(noised)
    own_theirs = [swap_cores(own)]
    others = jnp.stack(first)
    wg_theirs, wu_theirs = swap_cores(gate_weight), swap_cores(up_weight)
    keep_theirs = swap_cores(block_keep)[0].transpose(0, 2, 1)
    chunks = pltpu.VMEM((8, 512, 512), BF)
    fewer = pltpu.VMEM((4, 512, 512), BF)
    gate, up, mine_t, theirs_t, down_t = pl.pallas_call(
        prepare_kernel,
        out_shape=[shaped((8, 512, 512))] * 2 + [shaped((4, 1024, 512))] * 2 + [shaped((8, 512, 512))],
        in_specs=[smem] * 3 + [ANY] * 5, out_specs=[VM] * 5,
        scratch_shapes=[chunks, chunks, chunks, fewer, fewer, pltpu.SemaphoreType.DMA((5, 8))],
        compiler_params=room(20), cost_estimate=cost(1e7, 3.5e7), name="prepare",
    )(place, keep, keep_theirs, wg, wu, wd, hbm(wg_theirs[0]), hbm(wu_theirs[0]))
    rest = [others] + [phase(others, 1, SHIFTS[i]) for i in (1, 2, 3)]
    own_theirs += [swap_cores(owns[i]) for i in (1, 2, 3)]
    rest_theirs = [swap_cores(rest[i]) for i in range(4)]
    mine, theirs = owns + rest, own_theirs + rest_theirs

    mine[0], next_noised = barrier((mine[0], next_noised))
    ggup, hid_t, xa, ca = pl.pallas_call(
        forward_kernel,
        out_shape=[shaped((rows, 1024)), shaped((512, rows))] + [shaped((8, rows, 512))] * 2,
        in_specs=[smem] + [VM] * 19, out_specs=[VM] * 4,
        scratch_shapes=[pltpu.VMEM((rows, 512), F32)] * 3,
        compiler_params=room(12), cost_estimate=cost(4.8e9, 2.4e7), name="forward",
    )(place, *mine, *theirs, gate, up, down_t)

    ggup_theirs = swap_cores(ggup)
    part = pl.pallas_call(
        mine_kernel, out_shape=shaped((4, rows, 512), F32), in_specs=[VM] * 2, out_specs=VM,
        compiler_params=room(4), cost_estimate=cost(1.6e9, 6e6), name="mine",
    )(ggup, mine_t)
    outs = list(pl.pallas_call(
        own_kernel, out_shape=[shaped((4, CAP, 512), F32)] + [shaped((4, CAP, 512))] * 3,
        in_specs=[smem] + [VM] * 3, out_specs=[VM] * 4,
        scratch_shapes=[pltpu.VMEM((4, rows, 512), F32)],
        compiler_params=room(8), cost_estimate=cost(1.6e9, 1.2e7), name="own",
    )(place, part, ggup_theirs, theirs_t))
    got = [phase(o, 0, d) for o, d in zip(outs[1:], SHIFTS[1:])]
    ggup, outs[0] = barrier((ggup, outs[0]))
    grad_gate, grad_up = pl.pallas_call(
        gate_up_kernel, out_shape=[shaped((4096, 512))] * 2,
        in_specs=[smem] + [VM] * 2, out_specs=[ANY] * 2,
        scratch_shapes=[chunks, chunks, pltpu.SemaphoreType.DMA((2, 8))],
        compiler_params=room(16), cost_estimate=cost(3.2e9, 1.2e7), name="gate_up",
    )(keep, xa, ggup)
    *got, grad_gate, grad_up = barrier((*got, grad_gate, grad_up))
    tiles = pl.pallas_call(
        sum_kernel, out_shape=[shaped((CAP, 512), F32)] + [shaped((CAP, 512))] * 3,
        in_specs=[smem] + [VM] * 4, out_specs=[VM] * 4,
        compiler_params=room(8), cost_estimate=cost(1e6, 2.5e6), name="sum",
    )(place, outs[0], *got)
    got = [phase(o, 1, d) for o, d in zip(tiles[1:], SHIFTS[1:])]
    share = (tiles[0] + sum(g.astype(F32) for g in got)).astype(BF)
    share, hid_t = barrier((share, hid_t))
    share = to_preceding(share)
    grad_down = pl.pallas_call(
        down_kernel, out_shape=shaped((512, 4096)),
        in_specs=[smem] + [VM] * 2, out_specs=ANY,
        scratch_shapes=[chunks, pltpu.SemaphoreType.DMA((8,))],
        compiler_params=room(8), cost_estimate=cost(1.6e9, 8e6), name="down",
    )(keep, ca, hid_t)
    share, grad_down = barrier((share, grad_down))
    strip = [share] + [along_x(share, d) for d in SHIFTS[1:]]
    handoff = pl.pallas_call(
        expand_kernel, out_shape=shaped((128, 4096)),
        in_specs=[smem] + [VM] * 9, out_specs=VM,
        compiler_params=room(8), cost_estimate=cost(1e8, 2e6), name="expand",
    )(place, next_noised, *strip, *[swap_cores(t) for t in strip])
    return (grad_gate[None], grad_up[None], grad_down[None], handoff[None])


def solution(mesh):
    placed = (
        P("section", "col", "row"),
        P("section", "col", "row"),
        P("section", "col"),
        P("section", None, ("row", "col")),
        P("section", None, ("row", "col")),
        P("section", ("row", "col"), None),
        P("section", None, None, ("row", "col")),
    )

    return jax.shard_map(
        on_device,
        mesh=mesh,
        in_specs=placed,
        out_specs=(
            P("section", None, ("row", "col")),
            P("section", None, ("row", "col")),
            P("section", ("row", "col"), None),
            P("section", "col", None),
        ),
        check_vma=False,
    )
```

```python
import jax
import jax.numpy as jnp
from jax import lax
from jax.experimental import pallas as pl
from jax.experimental.pallas import tpu as pltpu
from jax.sharding import PartitionSpec as P


BF = jnp.bfloat16
F32 = jnp.float32
CAP = 96
SHIFTS = (0, 1, -1, 2)
ANY = pl.BlockSpec(memory_space=pl.ANY)
VM = pl.BlockSpec(memory_space=pltpu.VMEM)


def cost(flops, nbytes):
    return pl.CostEstimate(flops=int(flops), bytes_accessed=int(nbytes), transcendentals=0)


def phase(array, which, by):
    pairs = []
    for x in range(4):
        for core in range(2):
            for y in range(4):
                along_x = (core == 0) == (which == 0)
                tx, ty = ((x + by) % 4, y) if along_x else (x, (y + by) % 4)
                pairs.append(((x * 2 + core) * 4 + y, (tx * 2 + core) * 4 + ty))
    return lax.ppermute(array, ("row", "col"), pairs)


def swap_cores(array):
    return lax.ppermute(array, "row", [(i, i ^ 1) for i in range(8)])


def hand_over(array, by):
    pairs = [(z * 8 + i, (z - 1) * 8 + (i + 2 * by) % 8) for z in range(1, 4) for i in range(8)]
    return lax.ppermute(array, ("section", "row"), pairs)


def along_x(array, by):
    return lax.ppermute(array, "row", [(i, (i + 2 * by) % 8) for i in range(8)])


def to_preceding(array):
    return lax.ppermute(array, "section", [(i, i - 1) for i in range(1, 4)])


def selector(noised):
    flags = noised.astype(F32)
    lower = lax.broadcasted_iota(jnp.int32, (128, 128), 0) <= lax.broadcasted_iota(jnp.int32, (128, 128), 1)
    rank = jnp.dot(
        jnp.broadcast_to(flags, (16, 128)).astype(BF), lower.astype(F32).astype(BF), preferred_element_type=F32
    )[0:1]
    slot = lax.broadcasted_iota(jnp.int32, (CAP, 128), 0).astype(F32) + 1.0
    return jnp.where(jnp.logical_and(slot == rank, flags > 0.5), 1.0, 0.0).astype(BF)


def compact_kernel(noised, tokens, cotangent, own):
    pick = selector(noised[...])
    own[0] = jnp.dot(pick, tokens[...], preferred_element_type=F32).astype(BF)
    own[1] = jnp.dot(pick, cotangent[...], preferred_element_type=F32).astype(BF)


def masked(weight, keep, which, model_block, transposed=False):
    rows = []
    for i in range(4):
        cols = []
        for j in range(4):
            f, h = (j, i) if transposed else (i, j)
            flag = keep[which, h, model_block * 4 + f].astype(F32).astype(BF)
            cols.append(weight[i * 128 : (i + 1) * 128, j * 128 : (j + 1) * 128] * flag)
        rows.append(jnp.concatenate(cols, axis=1))
    return jnp.concatenate(rows, axis=0)


def prepare_kernel(
    place, keep, keep_theirs, wg, wu, wd, wg_theirs, wu_theirs,
    gate, up, mine_t, theirs_t, down_t, in_g, in_u, in_d, in_tg, in_tu, sem,
):
    base = place[1] * 4

    def block(i):
        return pl.ds(pl.multiple_of(i * 512, 512), 512)

    def copies(i):
        return [
            pltpu.make_async_copy(wg.at[block(i)], in_g.at[i], sem.at[0, i]),
            pltpu.make_async_copy(wu.at[block(i)], in_u.at[i], sem.at[1, i]),
            pltpu.make_async_copy(wd.at[:, block(i)], in_d.at[i], sem.at[2, i]),
        ]

    def their_copies(i):
        return [
            pltpu.make_async_copy(wg_theirs.at[block(base + i)], in_tg.at[i], sem.at[3, i]),
            pltpu.make_async_copy(wu_theirs.at[block(base + i)], in_tu.at[i], sem.at[4, i]),
        ]

    for i in range(8):
        for copy in copies(i):
            copy.start()
    for i in range(4):
        for copy in their_copies(i):
            copy.start()

    def step(i, carry):
        for copy in copies(i):
            copy.wait()
        at = (lax.rem(i, 2), block(i // 2))
        gate[at] = masked(in_g.at[i], keep, 0, i)
        up[at] = masked(in_u.at[i], keep, 1, i)
        down_t[at] = masked(in_d.at[i], keep, 2, i, True).T
        return carry

    lax.fori_loop(0, 8, step, 0)

    def their_step(i, carry):
        for copy in their_copies(i):
            copy.wait()
        at = (lax.rem(i, 2), block((base + i) // 2))
        mine_t[i, 0:512] = gate[at].T
        mine_t[i, 512:1024] = up[at].T
        theirs_t[i, 0:512] = masked(in_tg.at[i], keep_theirs, 0, base + i).T
        theirs_t[i, 512:1024] = masked(in_tu.at[i], keep_theirs, 1, base + i).T
        return carry

    lax.fori_loop(0, 4, their_step, 0)


def assemble(place, other, blocks, xs, cs):
    x, core, y = place[0], place[1], place[2]
    for i in range(4):
        for j in range(4):
            first, second = SHIFTS[j], SHIFTS[i]
            even = (core ^ other) == 0
            bx = lax.rem(x + 4 - jnp.where(even, first, second), 4)
            by = lax.rem(y + 4 - jnp.where(even, second, first), 4)
            at = (pl.ds(pl.multiple_of(by * CAP, CAP), CAP), pl.ds(pl.multiple_of(bx * 512, 512), 512))
            pair = blocks[i] if j == 0 else blocks[4 + i].at[j - 1]
            xs[at] = pair[0]
            cs[at] = pair[1]


def first_kernel(place, *refs):
    blocks, weights, (xs, cs), sums = refs[:8], refs[8:11], refs[11:13], refs[13:]
    assemble(place, 0, blocks, xs, cs)
    for total, left, weight in zip(sums, (xs, xs, cs), weights):
        for n in (slice(0, 256), slice(256, 512)):
            total[:, n] = jnp.dot(left[...], weight[place[1], :, n], preferred_element_type=F32)


def second_kernel(place, *refs):
    blocks, weights, before, (ggup, hid_t, xs, cs) = refs[:8], refs[8:11], refs[11:14], refs[14:]
    assemble(place, 1, blocks, xs, cs)
    for k in range(2):
        n = slice(k * 256, (k + 1) * 256)
        g, u, gh = (
            total[:, n] + jnp.dot(left[...], weight[1 - place[1], :, n], preferred_element_type=F32)
            for total, left, weight in zip(before, (xs, xs, cs), weights)
        )
        sig = 1.0 / (1.0 + jnp.exp(-g))
        silu = g * sig
        ggup[:, n] = (gh * u * sig * (1.0 + g * (1.0 - sig))).astype(BF)
        ggup[:, 512 + k * 256 : 768 + k * 256] = (gh * silu).astype(BF)
        hid_t[n] = (silu * u).astype(BF).T


def mine_kernel(mine, mine_t, out):
    def step(q, carry):
        out[q] = jnp.dot(mine[...], mine_t[q], preferred_element_type=F32)
        return carry

    lax.fori_loop(0, 4, step, 0)


def own_kernel(place, part, theirs, theirs_t, o0, o1, o2, o3, full):
    x, core, y = place[0], place[1], place[2]

    def step(q, carry):
        full[q] = (part[q] + jnp.dot(theirs[...], theirs_t[q], preferred_element_type=F32)).astype(BF)
        return carry

    lax.fori_loop(0, 4, step, 0)
    for shift, out in zip(SHIFTS, (o0, o1, o2, o3)):
        for t in range(4):
            q = jnp.where(core == 0, lax.rem(x + 4 + shift, 4), t)
            c = jnp.where(core == 0, t, lax.rem(y + 4 + shift, 4))
            out[t] = full[q, pl.ds(pl.multiple_of(c * CAP, CAP), CAP)]


def sum_kernel(place, own, r1, r2, r3, o0, o1, o2, o3):
    base = jnp.where(place[1] == 0, place[2], place[0])
    for shift, out in zip(SHIFTS, (o0, o1, o2, o3)):
        t = lax.rem(base + 4 + shift, 4)
        total = own[t].astype(F32) + r1[t].astype(F32) + r2[t].astype(F32) + r3[t].astype(F32)
        out[...] = total.astype(out.dtype)


def pick_kernel(noised, out):
    out[...] = selector(noised[...]).astype(F32).T.astype(BF)


def expand_kernel(place, pick, t0, t1, t2, t3, u0, u1, u2, u3, out, buf, sem):
    x, core = place[0], place[1]
    copies = []
    for other, tiles in ((0, (t0, t1, t2, t3)), (1, (u0, u1, u2, u3))):
        for i, tile in enumerate(tiles):
            n = other * 4 + i
            column = ((core ^ other) * 4 + lax.rem(x + 4 - SHIFTS[i], 4)) * 512
            buf[n] = jnp.dot(pick[...], tile[...], preferred_element_type=F32).astype(BF)
            copy = pltpu.make_async_copy(buf.at[n], out.at[:, pl.ds(pl.multiple_of(column, 512), 512)], sem.at[n])
            copy.start()
            copies.append(copy)
    for copy in copies:
        copy.wait()


def gate_up_kernel(place, keep, x0, x1, ggup, gg, gu, buf_g, buf_u, sem):
    def copies(r):
        rows = pl.ds(pl.multiple_of(r * 512, 512), 512)
        return [
            pltpu.make_async_copy(buf_g.at[r], gg.at[rows], sem.at[0, r]),
            pltpu.make_async_copy(buf_u.at[r], gu.at[rows], sem.at[1, r]),
        ]

    for other, xs in ((0, x0), (1, x1)):

        def step(bx, carry, xs=xs, parity=place[1] ^ other):
            r = bx * 2 + parity
            value = jnp.dot(xs[:, pl.ds(pl.multiple_of(bx * 512, 512), 512)].T, ggup[...], preferred_element_type=F32).astype(BF)
            buf_g[r] = masked(value[:, 0:512], keep, 0, r)
            buf_u[r] = masked(value[:, 512:1024], keep, 1, r)
            for copy in copies(r):
                copy.start()
            return carry

        lax.fori_loop(0, 4, step, 0)
    for r in range(8):
        for copy in copies(r):
            copy.wait()


def down_kernel(place, keep, c0, c1, hid_t, gd, buf, sem):
    def copy(r):
        return pltpu.make_async_copy(buf.at[r], gd.at[:, pl.ds(pl.multiple_of(r * 512, 512), 512)], sem.at[r])

    for other, cs in ((0, c0), (1, c1)):

        def step(bx, carry, cs=cs, parity=place[1] ^ other):
            r = bx * 2 + parity
            value = jnp.dot(hid_t[...], cs[:, pl.ds(pl.multiple_of(bx * 512, 512), 512)], preferred_element_type=F32).astype(BF)
            buf[r] = masked(value, keep, 2, r, True)
            copy(r).start()
            return carry

        lax.fori_loop(0, 4, step, 0)
    for r in range(8):
        copy(r).wait()


def shaped(shape, dtype=BF):
    return jax.ShapeDtypeStruct(shape, dtype)


def hbm(array):
    return pltpu.with_memory_space_constraint(array, pltpu.HBM)


def on_device(tokens, cotangent, noised, gate_weight, up_weight, down_weight, block_keep):
    row = lax.axis_index("row")
    place = jnp.stack([row // 2, row % 2, lax.axis_index("col")]).astype(jnp.int32)
    keep = block_keep[0].transpose(0, 2, 1)
    wg, wu, wd = (hbm(w[0]) for w in (gate_weight, up_weight, down_weight))
    rows = 4 * CAP
    smem = pl.BlockSpec(memory_space=pltpu.SMEM)

    def room(mib):
        return pltpu.CompilerParams(vmem_limit_bytes=mib << 20)

    own = pl.pallas_call(
        compact_kernel, out_shape=shaped((2, CAP, 512)), in_specs=[VM] * 3, out_specs=VM,
        compiler_params=room(4), cost_estimate=cost(5e7, 5e5), name="compact",
    )(*(hbm(v) for v in (noised, tokens[0], cotangent[0])))
    first = [phase(own, 0, SHIFTS[i]) for i in (1, 2, 3)]
    owns = [own] + [phase(own, 1, SHIFTS[i]) for i in (1, 2, 3)]
    next_noised = to_preceding(noised)
    own_theirs = [swap_cores(own)]
    others = jnp.stack(first)
    wg_theirs, wu_theirs = swap_cores(gate_weight), swap_cores(up_weight)
    keep_theirs = swap_cores(block_keep)[0].transpose(0, 2, 1)
    chunks = pltpu.VMEM((8, 512, 512), BF)
    fewer = pltpu.VMEM((4, 512, 512), BF)
    gate, up, mine_t, theirs_t, down_t = pl.pallas_call(
        prepare_kernel,
        out_shape=[shaped((2, 2048, 512))] * 2 + [shaped((4, 1024, 512))] * 2 + [shaped((2, 2048, 512))],
        in_specs=[smem] * 3 + [ANY] * 5, out_specs=[VM] * 5,
        scratch_shapes=[chunks, chunks, chunks, fewer, fewer, pltpu.SemaphoreType.DMA((5, 8))],
        compiler_params=room(20), cost_estimate=cost(1e7, 3.5e7), name="prepare",
    )(place, keep, keep_theirs, wg, wu, wd, hbm(wg_theirs[0]), hbm(wu_theirs[0]))
    rest = [others] + [phase(others, 1, SHIFTS[i]) for i in (1, 2, 3)]
    own_theirs += [swap_cores(owns[i]) for i in (1, 2, 3)]
    rest_theirs = [swap_cores(rest[i]) for i in range(4)]
    mine, theirs = owns + rest, own_theirs + rest_theirs

    half = shaped((rows, 2048))
    total = shaped((rows, 512), F32)
    x0, c0, *sums = pl.pallas_call(
        first_kernel, out_shape=[half] * 2 + [total] * 3,
        in_specs=[smem] + [VM] * 11, out_specs=[VM] * 5,
        compiler_params=room(8), cost_estimate=cost(2.4e9, 1.2e7), name="first",
    )(place, *mine, gate, up, down_t)
    ggup, hid_t, x1, c1 = pl.pallas_call(
        second_kernel, out_shape=[shaped((rows, 1024)), shaped((512, rows)), half, half],
        in_specs=[smem] + [VM] * 14, out_specs=[VM] * 4,
        compiler_params=room(10), cost_estimate=cost(2.4e9, 1.2e7), name="second",
    )(place, *theirs, gate, up, down_t, *sums)

    ggup_theirs = swap_cores(ggup)
    part = pl.pallas_call(
        mine_kernel, out_shape=shaped((4, rows, 512), F32), in_specs=[VM] * 2, out_specs=VM,
        compiler_params=room(4), cost_estimate=cost(1.6e9, 6e6), name="mine",
    )(ggup, mine_t)
    outs = list(pl.pallas_call(
        own_kernel, out_shape=[shaped((4, CAP, 512))] * 4,
        in_specs=[smem] + [VM] * 3, out_specs=[VM] * 4,
        scratch_shapes=[pltpu.VMEM((4, rows, 512), BF)],
        compiler_params=room(8), cost_estimate=cost(1.6e9, 1.2e7), name="own",
    )(place, part, ggup_theirs, theirs_t))
    got = [phase(outs[i], 0, SHIFTS[i]) for i in (1, 2, 3)]
    grad_gate, grad_up = pl.pallas_call(
        gate_up_kernel, out_shape=[shaped((4096, 512))] * 2,
        in_specs=[smem] * 2 + [VM] * 3, out_specs=[ANY] * 2,
        scratch_shapes=[chunks, chunks, pltpu.SemaphoreType.DMA((2, 8))],
        compiler_params=room(16), cost_estimate=cost(3.2e9, 1.2e7), name="gate_up",
    )(place, keep, x0, x1, ggup)
    tiles = pl.pallas_call(
        sum_kernel, out_shape=[shaped((CAP, 512), F32)] + [shaped((CAP, 512))] * 3,
        in_specs=[smem] + [VM] * 4, out_specs=[VM] * 4,
        compiler_params=room(8), cost_estimate=cost(1e6, 2.5e6), name="sum",
    )(place, outs[0], *got)
    got = [phase(tiles[i], 1, SHIFTS[i]) for i in (1, 2, 3)]
    grad_down = pl.pallas_call(
        down_kernel, out_shape=shaped((512, 4096)),
        in_specs=[smem] * 2 + [VM] * 3, out_specs=ANY,
        scratch_shapes=[chunks, pltpu.SemaphoreType.DMA((8,))],
        compiler_params=room(8), cost_estimate=cost(1.6e9, 8e6), name="down",
    )(place, keep, c0, c1, hid_t)
    share = (tiles[0] + sum(g.astype(F32) for g in got)).astype(BF)
    near, far = hand_over(share, 0), hand_over(share, 2)
    strip = [near, along_x(near, 1), along_x(near, -1), far]
    strip += [swap_cores(strip[i]) for i in range(4)]
    pick = pl.pallas_call(
        pick_kernel, out_shape=shaped((128, CAP)), in_specs=[VM], out_specs=VM,
        compiler_params=room(4), cost_estimate=cost(1e7, 1e5), name="pick",
    )(next_noised)
    handoff = pl.pallas_call(
        expand_kernel, out_shape=shaped((128, 4096)),
        in_specs=[smem] + [VM] * 9, out_specs=ANY,
        scratch_shapes=[pltpu.VMEM((8, 128, 512), BF), pltpu.SemaphoreType.DMA((8,))],
        compiler_params=room(8), cost_estimate=cost(1e8, 2e6), name="expand",
    )(place, pick, *strip)
    return (grad_gate[None], grad_up[None], grad_down[None], handoff[None])


def solution(mesh):
    placed = (
        P("section", "col", "row"),
        P("section", "col", "row"),
        P("section", "col"),
        P("section", None, ("row", "col")),
        P("section", None, ("row", "col")),
        P("section", ("row", "col"), None),
        P("section", None, None, ("row", "col")),
    )

    return jax.shard_map(
        on_device,
        mesh=mesh,
        in_specs=placed,
        out_specs=(
            P("section", None, ("row", "col")),
            P("section", None, ("row", "col")),
            P("section", ("row", "col"), None),
            P("section", "col", None),
        ),
        check_vma=False,
    )
```

```python
import jax
import jax.numpy as jnp
from jax import lax
from jax.experimental import pallas as pl
from jax.experimental.pallas import tpu as pltpu
from jax.sharding import PartitionSpec as P


BF = jnp.bfloat16
F32 = jnp.float32
CAP = 96
SHIFTS = (0, 1, -1, 2)
ANY = pl.BlockSpec(memory_space=pl.ANY)
VM = pl.BlockSpec(memory_space=pltpu.VMEM)


def cost(flops, nbytes):
    return pl.CostEstimate(flops=int(flops), bytes_accessed=int(nbytes), transcendentals=0)


def phase(array, which, by):
    pairs = []
    for x in range(4):
        for core in range(2):
            for y in range(4):
                along_x = (core == 0) == (which == 0)
                tx, ty = ((x + by) % 4, y) if along_x else (x, (y + by) % 4)
                pairs.append(((x * 2 + core) * 4 + y, (tx * 2 + core) * 4 + ty))
    return lax.ppermute(array, ("row", "col"), pairs)


def swap_cores(array):
    return lax.ppermute(array, "row", [(i, i ^ 1) for i in range(8)])


def hand_over(array, by):
    pairs = [(z * 8 + i, (z - 1) * 8 + (i + 2 * by) % 8) for z in range(1, 4) for i in range(8)]
    return lax.ppermute(array, ("section", "row"), pairs)


def along_x(array, by):
    return lax.ppermute(array, "row", [(i, (i + 2 * by) % 8) for i in range(8)])


def to_preceding(array):
    return lax.ppermute(array, "section", [(i, i - 1) for i in range(1, 4)])


def selector(noised):
    flags = noised.astype(F32)
    lower = lax.broadcasted_iota(jnp.int32, (128, 128), 0) <= lax.broadcasted_iota(jnp.int32, (128, 128), 1)
    rank = jnp.dot(
        jnp.broadcast_to(flags, (16, 128)).astype(BF), lower.astype(F32).astype(BF), preferred_element_type=F32
    )[0:1]
    slot = lax.broadcasted_iota(jnp.int32, (CAP, 128), 0).astype(F32) + 1.0
    return jnp.where(jnp.logical_and(slot == rank, flags > 0.5), 1.0, 0.0).astype(BF)


def compact_kernel(noised, tokens, cotangent, own):
    pick = selector(noised[...])
    own[0] = jnp.dot(pick, tokens[...], preferred_element_type=F32).astype(BF)
    own[1] = jnp.dot(pick, cotangent[...], preferred_element_type=F32).astype(BF)


def masked(weight, keep, which, model_block, transposed=False):
    rows = []
    for i in range(4):
        cols = []
        for j in range(4):
            f, h = (j, i) if transposed else (i, j)
            flag = keep[which, h, model_block * 4 + f].astype(F32).astype(BF)
            cols.append(weight[i * 128 : (i + 1) * 128, j * 128 : (j + 1) * 128] * flag)
        rows.append(jnp.concatenate(cols, axis=1))
    return jnp.concatenate(rows, axis=0)


def prepare_kernel(
    place, keep, keep_theirs, wg, wu, wd, wg_theirs, wu_theirs,
    gate, up, mine_t, theirs_t, down_t, in_g, in_u, in_d, in_tg, in_tu, sem,
):
    base = place[1] * 4

    def block(i):
        return pl.ds(pl.multiple_of(i * 512, 512), 512)

    def copies(i):
        return [
            pltpu.make_async_copy(wg.at[block(i)], in_g.at[i], sem.at[0, i]),
            pltpu.make_async_copy(wu.at[block(i)], in_u.at[i], sem.at[1, i]),
            pltpu.make_async_copy(wd.at[:, block(i)], in_d.at[i], sem.at[2, i]),
        ]

    def their_copies(i):
        return [
            pltpu.make_async_copy(wg_theirs.at[block(base + i)], in_tg.at[i], sem.at[3, i]),
            pltpu.make_async_copy(wu_theirs.at[block(base + i)], in_tu.at[i], sem.at[4, i]),
        ]

    for i in range(8):
        for copy in copies(i):
            copy.start()
    for i in range(4):
        for copy in their_copies(i):
            copy.start()

    def step(i, carry):
        for copy in copies(i):
            copy.wait()
        at = (lax.rem(i, 2), block(i // 2))
        gate[at] = masked(in_g.at[i], keep, 0, i)
        up[at] = masked(in_u.at[i], keep, 1, i)
        down_t[at] = masked(in_d.at[i], keep, 2, i, True).T
        return carry

    lax.fori_loop(0, 8, step, 0)

    def their_step(i, carry):
        for copy in their_copies(i):
            copy.wait()
        at = (lax.rem(i, 2), block((base + i) // 2))
        mine_t[i, 0:512] = gate[at].T
        mine_t[i, 512:1024] = up[at].T
        theirs_t[i, 0:512] = masked(in_tg.at[i], keep_theirs, 0, base + i).T
        theirs_t[i, 512:1024] = masked(in_tu.at[i], keep_theirs, 1, base + i).T
        return carry

    lax.fori_loop(0, 4, their_step, 0)


def assemble(place, other, blocks, xs, cs):
    x, core, y = place[0], place[1], place[2]
    for i in range(4):
        for j in range(4):
            first, second = SHIFTS[j], SHIFTS[i]
            even = (core ^ other) == 0
            bx = lax.rem(x + 4 - jnp.where(even, first, second), 4)
            by = lax.rem(y + 4 - jnp.where(even, second, first), 4)
            at = (pl.ds(pl.multiple_of(by * CAP, CAP), CAP), pl.ds(pl.multiple_of(bx * 512, 512), 512))
            pair = blocks[i] if j == 0 else blocks[4 + i].at[j - 1]
            xs[at] = pair[0]
            cs[at] = pair[1]


def first_kernel(place, *refs):
    blocks, weights, (xs, cs), sums = refs[:8], refs[8:11], refs[11:13], refs[13:]
    assemble(place, 0, blocks, xs, cs)
    for total, left, weight in zip(sums, (xs, xs, cs), weights):
        for n in (slice(0, 256), slice(256, 512)):
            total[:, n] = jnp.dot(left[...], weight[place[1], :, n], preferred_element_type=F32)


def second_kernel(place, *refs):
    blocks, weights, before, (ggup, hid_t, xs, cs) = refs[:8], refs[8:11], refs[11:14], refs[14:]
    assemble(place, 1, blocks, xs, cs)
    for k in range(2):
        n = slice(k * 256, (k + 1) * 256)
        g, u, gh = (
            total[:, n] + jnp.dot(left[...], weight[1 - place[1], :, n], preferred_element_type=F32)
            for total, left, weight in zip(before, (xs, xs, cs), weights)
        )
        sig = 1.0 / (1.0 + jnp.exp(-g))
        silu = g * sig
        ggup[:, n] = (gh * u * sig * (1.0 + g * (1.0 - sig))).astype(BF)
        ggup[:, 512 + k * 256 : 768 + k * 256] = (gh * silu).astype(BF)
        hid_t[n] = (silu * u).astype(BF).T


def mine_kernel(mine, mine_t, out):
    for q in range(4):
        out[q] = jnp.dot(mine[...], mine_t[q], preferred_element_type=F32)


def own_kernel(place, part, theirs, theirs_t, o0, o1, o2, o3, full):
    x, core, y = place[0], place[1], place[2]
    for q in range(4):
        full[q] = (part[q] + jnp.dot(theirs[...], theirs_t[q], preferred_element_type=F32)).astype(BF)
    for shift, out in zip(SHIFTS, (o0, o1, o2, o3)):
        for t in range(4):
            q = jnp.where(core == 0, lax.rem(x + 4 + shift, 4), t)
            c = jnp.where(core == 0, t, lax.rem(y + 4 + shift, 4))
            out[t] = full[q, pl.ds(pl.multiple_of(c * CAP, CAP), CAP)]


def sum_kernel(place, own, r1, r2, r3, o0, o1, o2, o3):
    base = jnp.where(place[1] == 0, place[2], place[0])
    for shift, out in zip(SHIFTS, (o0, o1, o2, o3)):
        t = lax.rem(base + 4 + shift, 4)
        total = own[t].astype(F32) + r1[t].astype(F32) + r2[t].astype(F32) + r3[t].astype(F32)
        out[...] = total.astype(out.dtype)


def pick_kernel(noised, out):
    out[...] = selector(noised[...]).astype(F32).T.astype(BF)


def expand_kernel(place, pick, t0, t1, t2, t3, u0, u1, u2, u3, out, buf, sem):
    x, core = place[0], place[1]
    copies = []
    for other, tiles in ((0, (t0, t1, t2, t3)), (1, (u0, u1, u2, u3))):
        for i, tile in enumerate(tiles):
            n = other * 4 + i
            column = ((core ^ other) * 4 + lax.rem(x + 4 - SHIFTS[i], 4)) * 512
            buf[n] = jnp.dot(pick[...], tile[...], preferred_element_type=F32).astype(BF)
            copy = pltpu.make_async_copy(buf.at[n], out.at[:, pl.ds(pl.multiple_of(column, 512), 512)], sem.at[n])
            copy.start()
            copies.append(copy)
    for copy in copies:
        copy.wait()


def gate_up_kernel(place, keep, x0, x1, ggup, gg, gu, buf_g, buf_u, sem):
    def copies(r):
        rows = pl.ds(pl.multiple_of(r * 512, 512), 512)
        return [
            pltpu.make_async_copy(buf_g.at[r], gg.at[rows], sem.at[0, r]),
            pltpu.make_async_copy(buf_u.at[r], gu.at[rows], sem.at[1, r]),
        ]

    for other, xs in ((0, x0), (1, x1)):

        def step(bx, carry, xs=xs, parity=place[1] ^ other):
            r = bx * 2 + parity
            value = jnp.dot(xs[:, pl.ds(pl.multiple_of(bx * 512, 512), 512)].T, ggup[...], preferred_element_type=F32).astype(BF)
            buf_g[r] = masked(value[:, 0:512], keep, 0, r)
            buf_u[r] = masked(value[:, 512:1024], keep, 1, r)
            for copy in copies(r):
                copy.start()
            return carry

        lax.fori_loop(0, 4, step, 0)
    for r in range(8):
        for copy in copies(r):
            copy.wait()


def down_kernel(place, keep, c0, c1, hid_t, gd, buf, sem):
    def copy(r):
        return pltpu.make_async_copy(buf.at[r], gd.at[:, pl.ds(pl.multiple_of(r * 512, 512), 512)], sem.at[r])

    for other, cs in ((0, c0), (1, c1)):

        def step(bx, carry, cs=cs, parity=place[1] ^ other):
            r = bx * 2 + parity
            value = jnp.dot(hid_t[...], cs[:, pl.ds(pl.multiple_of(bx * 512, 512), 512)], preferred_element_type=F32).astype(BF)
            buf[r] = masked(value, keep, 2, r, True)
            copy(r).start()
            return carry

        lax.fori_loop(0, 4, step, 0)
    for r in range(8):
        copy(r).wait()


def shaped(shape, dtype=BF):
    return jax.ShapeDtypeStruct(shape, dtype)


def hbm(array):
    return pltpu.with_memory_space_constraint(array, pltpu.HBM)


def on_device(tokens, cotangent, noised, gate_weight, up_weight, down_weight, block_keep):
    row = lax.axis_index("row")
    place = jnp.stack([row // 2, row % 2, lax.axis_index("col")]).astype(jnp.int32)
    keep = block_keep[0].transpose(0, 2, 1)
    wg, wu, wd = (hbm(w[0]) for w in (gate_weight, up_weight, down_weight))
    rows = 4 * CAP
    smem = pl.BlockSpec(memory_space=pltpu.SMEM)

    def room(mib):
        return pltpu.CompilerParams(vmem_limit_bytes=mib << 20)

    own = pl.pallas_call(
        compact_kernel, out_shape=shaped((2, CAP, 512)), in_specs=[VM] * 3, out_specs=VM,
        compiler_params=room(4), cost_estimate=cost(5e7, 5e5), name="compact",
    )(*(hbm(v) for v in (noised, tokens[0], cotangent[0])))
    first = [phase(own, 0, SHIFTS[i]) for i in (1, 2, 3)]
    owns = [own] + [phase(own, 1, SHIFTS[i]) for i in (1, 2, 3)]
    next_noised = to_preceding(noised)
    own_theirs = [swap_cores(own)]
    others = jnp.stack(first)
    wg_theirs, wu_theirs = swap_cores(gate_weight), swap_cores(up_weight)
    keep_theirs = swap_cores(block_keep)[0].transpose(0, 2, 1)
    chunks = pltpu.VMEM((8, 512, 512), BF)
    fewer = pltpu.VMEM((4, 512, 512), BF)
    gate, up, mine_t, theirs_t, down_t = pl.pallas_call(
        prepare_kernel,
        out_shape=[shaped((2, 2048, 512))] * 2 + [shaped((4, 1024, 512))] * 2 + [shaped((2, 2048, 512))],
        in_specs=[smem] * 3 + [ANY] * 5, out_specs=[VM] * 5,
        scratch_shapes=[chunks, chunks, chunks, fewer, fewer, pltpu.SemaphoreType.DMA((5, 8))],
        compiler_params=room(20), cost_estimate=cost(1e7, 3.5e7), name="prepare",
    )(place, keep, keep_theirs, wg, wu, wd, hbm(wg_theirs[0]), hbm(wu_theirs[0]))
    rest = [others] + [phase(others, 1, SHIFTS[i]) for i in (1, 2, 3)]
    own_theirs += [swap_cores(owns[i]) for i in (1, 2, 3)]
    rest_theirs = [swap_cores(rest[i]) for i in range(4)]
    mine, theirs = owns + rest, own_theirs + rest_theirs

    half = shaped((rows, 2048))
    total = shaped((rows, 512), F32)
    x0, c0, *sums = pl.pallas_call(
        first_kernel, out_shape=[half] * 2 + [total] * 3,
        in_specs=[smem] + [VM] * 11, out_specs=[VM] * 5,
        compiler_params=room(8), cost_estimate=cost(2.4e9, 1.2e7), name="first",
    )(place, *mine, gate, up, down_t)
    ggup, hid_t, x1, c1 = pl.pallas_call(
        second_kernel, out_shape=[shaped((rows, 1024)), shaped((512, rows)), half, half],
        in_specs=[smem] + [VM] * 14, out_specs=[VM] * 4,
        compiler_params=room(10), cost_estimate=cost(2.4e9, 1.2e7), name="second",
    )(place, *theirs, gate, up, down_t, *sums)

    ggup_theirs = swap_cores(ggup)
    part = pl.pallas_call(
        mine_kernel, out_shape=shaped((4, rows, 512), F32), in_specs=[VM] * 2, out_specs=VM,
        compiler_params=room(4), cost_estimate=cost(1.6e9, 6e6), name="mine",
    )(ggup, mine_t)
    outs = list(pl.pallas_call(
        own_kernel, out_shape=[shaped((4, CAP, 512))] * 4,
        in_specs=[smem] + [VM] * 3, out_specs=[VM] * 4,
        scratch_shapes=[pltpu.VMEM((4, rows, 512), BF)],
        compiler_params=room(8), cost_estimate=cost(1.6e9, 1.2e7), name="own",
    )(place, part, ggup_theirs, theirs_t))
    got = [phase(outs[i], 0, SHIFTS[i]) for i in (1, 2, 3)]
    grad_gate, grad_up = pl.pallas_call(
        gate_up_kernel, out_shape=[shaped((4096, 512))] * 2,
        in_specs=[smem] * 2 + [VM] * 3, out_specs=[ANY] * 2,
        scratch_shapes=[chunks, chunks, pltpu.SemaphoreType.DMA((2, 8))],
        compiler_params=room(16), cost_estimate=cost(3.2e9, 1.2e7), name="gate_up",
    )(place, keep, x0, x1, ggup)
    tiles = pl.pallas_call(
        sum_kernel, out_shape=[shaped((CAP, 512), F32)] + [shaped((CAP, 512))] * 3,
        in_specs=[smem] + [VM] * 4, out_specs=[VM] * 4,
        compiler_params=room(8), cost_estimate=cost(1e6, 2.5e6), name="sum",
    )(place, outs[0], *got)
    got = [phase(tiles[i], 1, SHIFTS[i]) for i in (1, 2, 3)]
    grad_down = pl.pallas_call(
        down_kernel, out_shape=shaped((512, 4096)),
        in_specs=[smem] * 2 + [VM] * 3, out_specs=ANY,
        scratch_shapes=[chunks, pltpu.SemaphoreType.DMA((8,))],
        compiler_params=room(8), cost_estimate=cost(1.6e9, 8e6), name="down",
    )(place, keep, c0, c1, hid_t)
    share = (tiles[0] + sum(g.astype(F32) for g in got)).astype(BF)
    near, far = hand_over(share, 0), hand_over(share, 2)
    strip = [near, along_x(near, 1), along_x(near, -1), far]
    strip += [swap_cores(strip[i]) for i in range(4)]
    pick = pl.pallas_call(
        pick_kernel, out_shape=shaped((128, CAP)), in_specs=[VM], out_specs=VM,
        compiler_params=room(4), cost_estimate=cost(1e7, 1e5), name="pick",
    )(next_noised)
    handoff = pl.pallas_call(
        expand_kernel, out_shape=shaped((128, 4096)),
        in_specs=[smem] + [VM] * 9, out_specs=ANY,
        scratch_shapes=[pltpu.VMEM((8, 128, 512), BF), pltpu.SemaphoreType.DMA((8,))],
        compiler_params=room(8), cost_estimate=cost(1e8, 2e6), name="expand",
    )(place, pick, *strip)
    return (grad_gate[None], grad_up[None], grad_down[None], handoff[None])


def solution(mesh):
    placed = (
        P("section", "col", "row"),
        P("section", "col", "row"),
        P("section", "col"),
        P("section", None, ("row", "col")),
        P("section", None, ("row", "col")),
        P("section", ("row", "col"), None),
        P("section", None, None, ("row", "col")),
    )

    return jax.shard_map(
        on_device,
        mesh=mesh,
        in_specs=placed,
        out_specs=(
            P("section", None, ("row", "col")),
            P("section", None, ("row", "col")),
            P("section", ("row", "col"), None),
            P("section", "col", None),
        ),
        check_vma=False,
    )
```
